32 devices in a mesh: row: 4 (over y, x), col: 8 (over z, core).
Axes of the slice: x: 2, y: 2, z: 4, core: 2. Of those that a mesh axis runs over, the one named last changes fastest.
Arguments:
- parent_entries: float32 [16384, 16384], P('row', 'col'), may hold values from -1.5 to 1.5
- children: float32 [6144, 12288], P('row', 'col'), may hold values from -1.5 to 1.5
- shift: float32 [16384], P('row'), may hold values from 24 to 48
- child_map: int32 [2, 96], replicated, may hold values from 0 to 255, as said below
Outputs:
- factored_front: float32 [16384, 16384], P('row', 'col')
The draws below stay inside these ranges and needn't reach their ends.
Inputs may be any that keep to these rules, and one draw needn't show every extreme that they name: `child_map`: row k sends child k's tiles to distinct parent tiles. For each child and each residue s modulo 4, the entries at positions congruent to s hold at most 8 values of any one residue modulo 4 and at most 8 of any one residue modulo 8, both bounds reached for every s; for each residue v modulo 4, exactly 24 entries of a row are congruent to v.
All inputs are finite; a program needn't handle non-finite values.
Results may differ from the reference program's by a relative error of at most 0.00005.
Values sent between devices are 32-bit elements; how exact they have to be, the bound alone decides.
A program may use at most 448 MiB of HBM per device.

```python
import math
import jax
import jax.numpy as jnp
from jax import lax

PARENT_ORDER = 16384
C = 6144
TILE = 64
ROWS_GRID = 4
COLS_GRID = 8
PBLOCKS = 256
CBLOCKS = 96
ELIMINATED_COLS = 512
GROUPS = 24
SLOTS = 8


def draw_child_map(key, part):
    rows_out = []
    ordinal = jnp.arange(CBLOCKS)
    group_of = ordinal // ROWS_GRID
    residue = ordinal % ROWS_GRID
    steps_idx = jnp.arange(GROUPS)
    spread = max(ROWS_GRID - 1, 1)
    for child in range(2):
        child_key = jax.random.fold_in(key, child + 11)
        key_lead, key_order, key_upper, key_slot = jax.random.split(child_key, 4)
        leading_row = jax.random.randint(key_lead, (), 0, ROWS_GRID)
        offsets = jnp.where(steps_idx < SLOTS, leading_row, (leading_row + 1 + (steps_idx - SLOTS) % spread) % ROWS_GRID)
        shuffle = jax.random.permutation(key_order, GROUPS)
        offset_of = offsets[shuffle]
        in_lead = shuffle < SLOTS
        dest_row = (residue + offset_of[group_of]) % ROWS_GRID
        upper_half = jax.random.randint(key_upper, (CBLOCKS,), 0, 2)
        upper_half = jnp.where(in_lead[group_of], 0, upper_half)
        dest_col = dest_row + ROWS_GRID * upper_half
        earlier = (dest_col[:, None] == dest_col[None, :]) & (ordinal[None, :] < ordinal[:, None])
        place_rank = jnp.sum(earlier.astype(jnp.int32), axis=1)
        levels = jax.random.permutation(key_slot, PBLOCKS // COLS_GRID)
        rows_out.append(levels[place_rank] * COLS_GRID + dest_col)
    return jnp.stack(rows_out).astype(jnp.int32)


def level_of(own_key, shape, cuts, smallest, high):
    def one(position, blocks):
        steps = jax.random.uniform(jax.random.fold_in(jax.random.fold_in(own_key, 6), position), (blocks,), jnp.float32, smallest / len(cuts), high / len(cuts))
        return jnp.repeat(jnp.exp(steps), shape[position] // blocks).reshape((-1,) + (1,) * (len(shape) - position - 1))

    factor_of = one(*cuts[0])
    for cut in cuts[1:]:
        factor_of = factor_of * one(*cut)
    return factor_of


def scatter_about(rng, extent, width, limit, cuts=(), kind=jnp.bfloat16):
    values = width * jax.random.normal(rng, extent, jnp.float32)
    if cuts:
        values = values * level_of(rng, extent, cuts, -0.22, 0.18)
    return jnp.clip(values, -limit, limit).astype(kind)


def setup_inputs(seed: int = 0) -> dict:
    streams_of = jax.random.split(jax.random.key(seed), 5)
    return {
        "parent_entries": scatter_about(streams_of[0], (PARENT_ORDER, PARENT_ORDER), 0.25, 1.5, ((0, 4), (1, 8)), jnp.float32),
        "children": scatter_about(streams_of[1], (C, 2 * C), 0.25, 1.5, ((0, 4), (1, 8)), jnp.float32),
        "shift": jnp.clip(jnp.exp(math.log(48.0) - 0.6931472 * jax.random.uniform(streams_of[2], (PARENT_ORDER,), jnp.float32) ** level_of(streams_of[2], (PARENT_ORDER,), ((0, 4),), -0.2, 0.2)), 24.0, 48.0),
        "child_map": draw_child_map(jax.random.fold_in(streams_of[4], 71), 0),
    }


def rows_natural(source, grid_size):
    count = source.shape[0]
    rest = source.shape[1:]
    shaped = source.reshape((grid_size, count // (grid_size * TILE), TILE) + rest)
    return jnp.swapaxes(shaped, 0, 1).reshape((count,) + rest)

def rows_storage(source, grid_size):
    count = source.shape[0]
    rest = source.shape[1:]
    shaped = source.reshape((count // (grid_size * TILE), grid_size, TILE) + rest)
    return jnp.swapaxes(shaped, 0, 1).reshape((count,) + rest)

def natural(source, row_grid, col_grid):
    return rows_natural(rows_natural(source, row_grid).T, col_grid).T

def storage(source, row_grid, col_grid):
    return rows_storage(rows_storage(source, row_grid).T, col_grid).T

def reference(parent_entries, children, shift, child_map):
    parent_front_matrix = natural(parent_entries, ROWS_GRID, COLS_GRID)
    diagonal = jnp.arange(PARENT_ORDER)
    parent_front_matrix = parent_front_matrix.at[diagonal, diagonal].add(rows_natural(shift, ROWS_GRID))
    front_tiles = parent_front_matrix.reshape(PBLOCKS, TILE, PBLOCKS, TILE)
    for child in range(2):
        block = natural(children[:, child * C:(child + 1) * C], ROWS_GRID, ROWS_GRID)
        child_tiles = block.reshape(CBLOCKS, TILE, CBLOCKS, TILE).transpose(0, 2, 1, 3)
        block_map = child_map[child]
        front_tiles = front_tiles.at[block_map[:, None], :, block_map[None, :], :].add(child_tiles)
    parent_front_matrix = front_tiles.reshape(PARENT_ORDER, PARENT_ORDER)
    leading_block = parent_front_matrix[:ELIMINATED_COLS, :ELIMINATED_COLS]
    pivot_block = jnp.linalg.cholesky((leading_block + leading_block.T) * 0.5)
    below_pivot_block = parent_front_matrix[ELIMINATED_COLS:, :ELIMINATED_COLS]
    lower_factor = jax.scipy.linalg.solve_triangular(pivot_block, below_pivot_block.T, lower=True).T
    schur_complement_block = parent_front_matrix[ELIMINATED_COLS:, ELIMINATED_COLS:] - jnp.dot(lower_factor, lower_factor.T, precision=lax.Precision.HIGHEST)
    upper_section = jnp.concatenate([pivot_block, jnp.zeros((ELIMINATED_COLS, PARENT_ORDER - ELIMINATED_COLS), jnp.float32)], axis=1)
    bottom_part = jnp.concatenate([lower_factor, schur_complement_block], axis=1)
    result = jnp.concatenate([upper_section, bottom_part], axis=0)
    return storage(result, ROWS_GRID, COLS_GRID)
```

```python
import jax
import jax.numpy as jnp
from jax import lax
from jax.experimental import pallas as pl
from jax.experimental.pallas import tpu as pltpu
from jax.sharding import PartitionSpec as P

TILE = 64


def from_root(value, axis, source):
    kept = jnp.where(lax.axis_index(axis) == source, value, 0).astype(value.dtype)
    return lax.psum(kept, axis)


def outgoing(block_map, sources, grid_size, own_index, slot_count):
    groups = block_map.shape[0] // sources
    block_table = jnp.take(block_map.reshape(groups, sources), own_index, axis=1)
    target = block_table % grid_size
    ordinal = jnp.arange(groups)
    earlier = (target[:, None] == target[None, :]) & (ordinal[None, :] < ordinal[:, None])
    earlier_count = jnp.sum(earlier.astype(jnp.int32), axis=1)
    picked = (target[None, :, None] == jnp.arange(grid_size)[:, None, None]) & (
        earlier_count[None, :, None] == jnp.arange(slot_count)[None, None, :]
    )
    return jnp.sum(jnp.where(picked, ordinal[None, :, None], 0), axis=1)


def incoming(block_map, sources, grid_size, own_index, slot_count):
    groups = block_map.shape[0] // sources
    block_table = block_map.reshape(groups, sources).T
    to_here = block_table % grid_size == own_index
    counts = to_here.astype(jnp.int32)
    earlier_count = jnp.cumsum(counts, axis=1) - counts
    picked = to_here[:, :, None] & (
        earlier_count[:, :, None] == jnp.arange(slot_count)[None, None, :]
    )
    present = jnp.any(picked, axis=1)
    target = jnp.sum(jnp.where(picked, block_table[:, :, None], 0), axis=1)
    return (present, target)


def compacted(block_map, grid_size, own_index, slot_count, groups):
    present, target = incoming(block_map, grid_size, grid_size, own_index, slot_count)
    flat_present = present.reshape(-1)
    flat_target = target.reshape(-1)
    counts = flat_present.astype(jnp.int32)
    position = jnp.cumsum(counts) - counts
    picked = flat_present[None, :] & (position[None, :] == jnp.arange(groups)[:, None])
    chosen = jnp.sum(jnp.where(picked, jnp.arange(flat_present.shape[0])[None, :], 0), axis=1)
    blocks = jnp.sum(jnp.where(picked, flat_target[None, :], 0), axis=1)
    return (chosen, blocks)


CHUNKS = 4


def lane_half(value, column, half):
    return jnp.where(column % 2 == half, value, pltpu.roll(value, TILE, 1))


def lane_pair(column):
    return pl.ds(pl.multiple_of((column // 2) * (2 * TILE), 2 * TILE), 2 * TILE)


def shuffle_columns(source, row_table, major_table, column_table, dests):
    majors, _, _, width = source.shape
    rows = row_table.shape[0]
    count = column_table.shape[0]
    per_dest = count // dests

    def body(row_ref, major_ref, column_ref, in_ref, out_ref):
        low = lax.broadcasted_iota(jnp.int32, (TILE, 2 * TILE), 1) < TILE
        for first in range(0, count, 2):
            halves = []
            for half in range(2):
                column = column_ref[first + half]
                value = in_ref[major_ref[first + half], 0, :, lane_pair(column)]
                halves.append(lane_half(value, column, half))
            place = first % per_dest
            out_ref[first // per_dest, 0, :, place * TILE : (place + 2) * TILE] = jnp.where(
                low, halves[0], halves[1]
            )

    return pl.pallas_call(
        body,
        out_shape=jax.ShapeDtypeStruct((dests, rows, TILE, per_dest * TILE), jnp.float32),
        grid_spec=pltpu.PrefetchScalarGridSpec(
            num_scalar_prefetch=3,
            grid=(rows,),
            in_specs=[
                pl.BlockSpec((majors, 1, TILE, width), lambda j, row, major, column: (0, row[j], 0, 0))
            ],
            out_specs=pl.BlockSpec(
                (dests, 1, TILE, per_dest * TILE), lambda j, row, major, column: (0, j, 0, 0)
            ),
        ),
        cost_estimate=pl.CostEstimate(
            flops=0, transcendentals=0, bytes_accessed=8 * rows * TILE * count * TILE
        ),
    )(row_table, major_table, column_table, source)


def extend_add(front, update, row_table, column_table):
    rows, _, width = update.shape
    cols_here = front.shape[1]

    def body(row_ref, column_ref, front_ref, update_ref, out_ref):
        out_ref[...] = front_ref[...]

        @pl.when(row_ref[pl.program_id(0)] >= 2)
        def _():
            upper = lax.broadcasted_iota(jnp.int32, (TILE, 2 * TILE), 1) // TILE
            for q in range(width // TILE):
                column = column_ref[q]

                @pl.when(column >= 1)
                def _():
                    first = (q // 2) * 2 * TILE
                    value = lane_half(update_ref[0, :, first : first + 2 * TILE], column, q % 2)
                    out_ref[:, lane_pair(column)] += jnp.where(upper == column % 2, value, 0.0)

    return pl.pallas_call(
        body,
        out_shape=jax.ShapeDtypeStruct(front.shape, jnp.float32),
        grid_spec=pltpu.PrefetchScalarGridSpec(
            num_scalar_prefetch=2,
            grid=(rows,),
            in_specs=[
                pl.BlockSpec((TILE, cols_here), lambda j, row, column: (row[j], 0)),
                pl.BlockSpec((1, TILE, width), lambda j, row, column: (j, 0, 0)),
            ],
            out_specs=pl.BlockSpec((TILE, cols_here), lambda j, row, column: (row[j], 0)),
        ),
        input_output_aliases={2: 0},
        cost_estimate=pl.CostEstimate(
            flops=rows * TILE * width,
            transcendentals=0,
            bytes_accessed=4 * rows * TILE * (2 * cols_here + width),
        ),
    )(row_table, column_table, front, update)


def local(parent_entries, children, shift, child_map):
    rows_here, cols_here = parent_entries.shape
    grid_rows = lax.axis_size("row")
    grid_cols = lax.axis_size("col")
    half_grid = grid_cols // 2
    row_index = lax.axis_index("row")
    col_index = lax.axis_index("col")
    child_now = col_index // half_grid
    half_col = col_index % half_grid
    child_width = children.shape[1]
    groups = children.shape[0] // TILE
    slot_count = groups // grid_rows + 2
    col_slots = slot_count + slot_count % 2
    row_blocks = rows_here // TILE
    own_map = jnp.take(child_map, child_now, axis=0)

    chosen_lists, row_lists, col_chosen, col_lists = [], [], [], []
    for child in range(2):
        chosen, blocks = compacted(child_map[child], grid_rows, row_index, slot_count, groups)
        chosen_lists.append(chosen)
        row_lists.append(blocks // grid_rows)
        chosen, blocks = compacted(child_map[child], half_grid, half_col, col_slots, groups)
        col_chosen.append(chosen)
        col_lists.append(jnp.where(blocks % grid_cols == col_index, blocks // grid_cols, -1))
    row_lists = jnp.stack(row_lists)
    col_lists = jnp.stack(col_lists)
    own_chosen = jnp.take(jnp.stack(chosen_lists), child_now, axis=0)
    own_col_chosen = jnp.take(jnp.stack(col_chosen), child_now, axis=0)

    first_sources = outgoing(own_map, grid_rows, grid_rows, row_index, slot_count)
    child_blocks = children.reshape(groups, TILE, child_width)
    outbound = jnp.take(child_blocks, first_sources.reshape(-1), axis=0, mode="clip").reshape(
        grid_rows, slot_count, TILE, child_width
    )
    arrived = lax.all_to_all(outbound, "row", split_axis=0, concat_axis=0, tiled=True)
    arrived = arrived.reshape(1, grid_rows * slot_count, TILE, child_width)

    owned = jnp.take(own_map.reshape(groups, half_grid), half_col, axis=1)
    leads = owned[:, None] == jnp.arange(grid_cols)[None, :]
    lead_source = jnp.sum(jnp.where(leads, jnp.arange(groups)[:, None], 0), axis=0)
    lead_strips = shuffle_columns(arrived, own_chosen, jnp.zeros_like(lead_source), lead_source, 1)
    lead_strips = lead_strips.reshape(groups * TILE, grid_cols * TILE).T.reshape(
        grid_cols, TILE, groups * TILE
    )
    lead_strips = jnp.where(jnp.any(leads, axis=0)[:, None, None], lead_strips, 0.0)
    lead_arrived = lax.all_to_all(lead_strips, "col", split_axis=0, concat_axis=0, tiled=True)

    second_sources = outgoing(own_map, half_grid, half_grid, half_col, col_slots).reshape(-1)
    halves = [list(range(half_grid)), list(range(half_grid, grid_cols))]
    swap = [(c, (c + half_grid) % grid_cols) for c in range(grid_cols)]
    step = groups // CHUNKS
    sends = []
    for chunk in range(CHUNKS):
        part = shuffle_columns(
            arrived,
            own_chosen[chunk * step : (chunk + 1) * step],
            jnp.zeros_like(second_sources),
            second_sources,
            half_grid,
        )
        sends.append(part)
    held = lax.optimization_barrier((lead_arrived, *sends))
    lead_arrived, sends = held[0], held[1:]
    own_parts = []
    for part in sends:
        got = lax.all_to_all(
            part, "col", split_axis=0, concat_axis=0, tiled=True, axis_index_groups=halves
        )
        own = shuffle_columns(
            got, jnp.arange(step), own_col_chosen // col_slots, own_col_chosen % col_slots, 1
        )[0]
        own_parts.append(own)

    lead_arrived = jnp.sum(lead_arrived.reshape(2, half_grid, TILE, groups * TILE), axis=1)
    row_ids = (
        (jnp.arange(row_blocks) * grid_rows + row_index)[:, None] * TILE + jnp.arange(TILE)
    ).reshape(rows_here)
    col_ids = (
        (jnp.arange(cols_here // TILE) * grid_cols + col_index)[:, None] * TILE + jnp.arange(TILE)
    ).reshape(cols_here)
    panel = parent_entries[:, :TILE] + jnp.where(
        row_ids[:, None] == col_ids[None, :TILE], shift[:, None], 0.0
    )
    panel = panel.reshape(row_blocks, TILE, TILE)
    for child in range(2):
        hits = jnp.arange(row_blocks)[:, None] == row_lists[child][None, :]
        source = jnp.sum(jnp.where(hits, jnp.arange(groups)[None, :], 0), axis=1)
        strip = lead_arrived[child].T.reshape(groups, TILE, TILE)
        strip = jnp.take(strip, source, axis=0, mode="clip")
        panel = panel + jnp.where(jnp.any(hits, axis=1)[:, None, None], strip, 0.0)
    panel = panel.reshape(rows_here, TILE)

    eliminated = TILE * grid_cols
    corner = panel[: 2 * TILE].reshape(1, 2 * TILE * TILE)
    corners = lax.all_gather(corner, ("row", "col"), axis=0, tiled=True)
    leading_block = (
        corners.reshape(grid_rows, grid_cols, 2, TILE, TILE)
        .transpose(2, 0, 3, 1, 4)
        .reshape(eliminated, eliminated)
    )
    gathered = lax.all_gather(panel.T, "col", axis=0, tiled=True)
    parity = col_index // grid_rows
    halves_t = gathered.reshape(eliminated, row_blocks // 2, 2, TILE)
    picked = lax.dynamic_index_in_dim(halves_t, parity, axis=2, keepdims=False).reshape(
        eliminated, cols_here
    )
    picked = from_root(picked, "row", col_index % grid_rows)
    half = CHUNKS // 2
    held = lax.optimization_barrier((leading_block, *own_parts[:half]))
    leading_block, own_parts[:half] = held[0], held[1:]
    pivot_block = jnp.linalg.cholesky((leading_block + leading_block.T) * 0.5)
    other_parts = [lax.ppermute(own, "col", swap) for own in own_parts[:half]]
    held = lax.optimization_barrier((pivot_block, other_parts[0], *own_parts[half:]))
    pivot_block, other_parts[0], own_parts[half:] = held[0], held[1], held[2:]
    other_parts += [lax.ppermute(own, "col", swap) for own in own_parts[half:]]
    solved = jax.scipy.linalg.solve_triangular(
        pivot_block, jnp.concatenate([gathered, picked], axis=1), lower=True
    )
    held = lax.optimization_barrier((solved, *other_parts[1:-1]))
    solved, other_parts[1:-1] = held[0], held[1:]
    factor_t, col_factor = solved[:, :rows_here], solved[:, rows_here:]
    own_pivot = jnp.concatenate(
        [
            lax.dynamic_slice_in_dim(pivot_block, row_index * TILE, TILE, 0),
            lax.dynamic_slice_in_dim(pivot_block, (row_index + grid_rows) * TILE, TILE, 0),
        ],
        axis=0,
    )
    factor_t = factor_t.at[:, : 2 * TILE].set(own_pivot.T)
    update = lax.dot_general(
        factor_t,
        col_factor,
        (((0,), (0,)), ((), ())),
        precision=lax.Precision.HIGH,
        preferred_element_type=jnp.float32,
    )
    result = parent_entries - update
    result = result + jnp.where(row_ids[:, None] == col_ids[None, :], shift[:, None], 0.0)
    panel_out = lax.dynamic_slice_in_dim(factor_t, col_index * TILE, TILE, 0).T
    result = jnp.where((jnp.arange(rows_here) < 2 * TILE)[:, None], 0.0, result)
    result = result.at[:, :TILE].set(panel_out)

    own_rows = jnp.take(row_lists, child_now, axis=0)
    other_rows = jnp.take(row_lists, 1 - child_now, axis=0)
    own_cols = jnp.take(col_lists, child_now, axis=0)
    other_cols = jnp.take(col_lists, 1 - child_now, axis=0)
    for parts, rows, cols in ((own_parts, own_rows, own_cols), (other_parts, other_rows, other_cols)):
        for chunk, part in enumerate(parts):
            result = extend_add(result, part, rows[chunk * step : (chunk + 1) * step], cols)
    return result


def solution(mesh):
    in_specs = (P("row", "col"), P("row", "col"), P("row"), P())
    out_specs = P("row", "col")
    return jax.shard_map(local, mesh=mesh, in_specs=in_specs, out_specs=out_specs, check_vma=False)
```
